32 devices in a mesh: section: 4 (over z), ep: 8 (over y, x, core).
Axes of the slice: x: 2, y: 2, z: 4, core: 2. Of those that a mesh axis runs over, the one named last changes fastest.
Arguments:
- flight_a: bfloat16 [4, 1024, 3584], P('section', 'ep'), may hold values from -6 to 6
- flight_b: bfloat16 [4, 1024, 3584], P('section', 'ep'), may hold values from -6 to 6
- routes_a: int32 [4, 1, 1024, 1], P('section', None, 'ep'), may hold values from 0 to 1; in each aligned block of 128 rows (0 to 127, 128 to 255, ..., all dimensions but the last counted through in order) at most 72 rows name the same one
- routes_b: int32 [4, 1, 1024, 1], P('section', None, 'ep'), may hold values from 0 to 1; in each aligned block of 128 rows (0 to 127, 128 to 255, ..., all dimensions but the last counted through in order) at most 72 rows name the same one
- scores_a: float32 [4, 1, 1024, 1], P('section', None, 'ep'), may hold values from 0.5 to 1.5
- scores_b: float32 [4, 1, 1024, 1], P('section', None, 'ep'), may hold values from 0.5 to 1.5
- norm_gain: float32 [4, 3584], P('section'), may hold values from 0.1 to 1.9
- w_gate: bfloat16 [4, 3584, 2048], P('section', None, 'ep'), may hold values from -0.09375 to 0.09375
- w_up: bfloat16 [4, 3584, 2048], P('section', None, 'ep'), may hold values from -0.09375 to 0.09375
- w_down: bfloat16 [4, 2048, 3584], P('section', 'ep'), may hold values from -0.1875 to 0.1875
Outputs:
- out_a: bfloat16 [4, 1024, 3584], P('section', 'ep')
- out_b: bfloat16 [4, 1024, 3584], P('section', 'ep')
The draws below stay inside these ranges and needn't reach their ends.
Inputs may be any that keep to these rules, and one draw needn't show every extreme that they name: `routes_a`: in each block of 128 rows that one device holds for one layer and step, no expert is named more than 72 times, a bound that some block reaches; a row never names one expert twice. `routes_b`: as for routes_a.
All inputs are finite; a program needn't handle non-finite values.
Results may differ from the reference program's by a relative error of at most 0.0054.
Values may be sent and summed in bfloat16 or wider, within the bound.
A program may use at most 128 MiB of HBM per device.

```python
import math
import jax
import jax.numpy as jnp
import numpy as np
from jax import lax

D = 3584
FFE = 1024
ES = 4
TOPK = 1
STEPS = 1
TOK_DEV = 128
EXPERTS = 2
CAP = 72
TOKENS = 1024
LAYERS = 4
N_EP = 8


def block_levels(stream_key, dims, split, smallest, largest):
    level, own = 1.0, jax.random.fold_in(stream_key, 6)
    for dim, parts in split:
        draws = jnp.exp(jax.random.uniform(jax.random.fold_in(own, dim), (parts,), jnp.float32, smallest / len(split), largest / len(split)))
        level = level * jnp.repeat(draws, dims[dim] // parts).reshape([-1 if axis == dim else 1 for axis in range(len(dims))])
    return level


def deal_out(rng, own, number, rows, number_of, top, most, skew):
    order = jax.random.permutation(rng, number_of)
    heavy_load, common = shares(number_of, rows * top, most, skew, True), shares(number_of, rows * top, most, skew, False)
    places = jnp.arange(number_of)

    def named(tallies, rotation):
        used = int((tallies > 0).sum())
        fixed = max(1, used // 4)
        passed = fixed + (places - fixed + rotation * (used - fixed)) % max(1, number_of - fixed)
        return jnp.zeros((number_of,), jnp.int32).at[order[jnp.where(places < fixed, places, passed)]].set(jnp.asarray(tallies, jnp.int32))

    tallies = jnp.where(number % 4 == 0, named(heavy_load, number // 4), named(common, number - number // 4 - 1))
    mixed = jax.random.permutation(jax.random.fold_in(own, 3), number_of)
    source_of, taker = mixed[0:number_of // 2 * 2:2], mixed[1:number_of // 2 * 2:2]
    margin = jnp.minimum(tallies[source_of] - 1, most - tallies[taker]) // 2
    margin = jnp.where((source_of == order[0]) | (taker == order[0]) | (tallies[taker] == 0), 0, jnp.maximum(margin, 0))
    passed = jax.random.randint(jax.random.fold_in(own, 4), (number_of // 2,), 0, 1 << 20) % (margin + 1)
    tallies = tallies.at[source_of].add(-passed).at[taker].add(passed)
    members = jnp.searchsorted(jnp.cumsum(tallies), jnp.arange(rows * top), side="right").astype(jnp.int32)
    listing = members.reshape(top, rows).T
    listing = listing[jax.random.permutation(jax.random.fold_in(own, 1), rows)]
    rotation = jax.random.randint(jax.random.fold_in(own, 2), (rows, 1), 0, top)
    return jnp.take_along_axis(listing, (jnp.arange(top)[None, :] + rotation) % top, axis=1)


def shares(count, total, bound, skew, full):
    portions = [(1 << 20) // math.isqrt(rank ** skew) + 1 for rank in range(1, count + 1)]
    largest = bound if full else min(bound, max(-(-total // count), total * portions[0] // sum(portions)))
    least = 1 if total - largest >= count - 1 else 0
    given, spare = [largest] + [least] * (count - 1), total - largest - least * (count - 1)
    while spare > 0:
        movable = [i for i in range(1, count) if given[i] < largest] or [i for i in range(1, count) if given[i] < bound]
        whole, budget = sum([portions[i] for i in movable]), spare
        for i in movable:
            extra = min(bound - given[i], max(1, budget * portions[i] // whole), spare)
            given[i] = given[i] + extra
            spare = spare - extra
    return np.array(given)


def normal_values(rng, dims, scale, most, cuts=(), kind=jnp.bfloat16):
    level = block_levels(rng, dims, cuts, -0.22, 0.18) if cuts else 1.0
    drawn = jax.random.normal(rng, dims, jnp.float32) * scale * level
    return jnp.minimum(jnp.maximum(drawn, -most), most).astype(kind)


def setup_inputs(seed: int = 0) -> dict:
    keys = jax.random.split(jax.random.key(seed), 11)
    flight_a = normal_values(keys[0], (LAYERS, TOKENS, D), 1.0, 6.0, ((0, 4), (1, 8)))
    flight_b = normal_values(keys[1], (LAYERS, TOKENS, D), 1.0, 6.0, ((0, 4), (1, 8)))
    routes_a_keys = jax.random.split(jax.random.fold_in(keys[2], 1), LAYERS * STEPS * TOKENS // TOK_DEV)
    routes_a_turns = jax.random.permutation(jax.random.fold_in(keys[2], 3), LAYERS * STEPS * TOKENS // TOK_DEV)
    routes_a = jax.vmap(lambda own, number: deal_out(jax.random.fold_in(keys[2], 2), own, number, TOK_DEV, EXPERTS, TOPK, CAP, 1))(routes_a_keys, routes_a_turns).reshape((LAYERS, STEPS, TOKENS, TOPK))
    routes_b_keys = jax.random.split(jax.random.fold_in(keys[3], 1), LAYERS * STEPS * TOKENS // TOK_DEV)
    routes_b_turns = jax.random.permutation(jax.random.fold_in(keys[3], 3), LAYERS * STEPS * TOKENS // TOK_DEV)
    routes_b = jax.vmap(lambda own, number: deal_out(jax.random.fold_in(keys[3], 2), own, number, TOK_DEV, EXPERTS, TOPK, CAP, 1))(routes_b_keys, routes_b_turns).reshape((LAYERS, STEPS, TOKENS, TOPK))
    scores_a = jnp.clip(0.5 + 1.0 * jax.random.uniform(keys[4], (LAYERS, STEPS, TOKENS, TOPK), jnp.float32) ** block_levels(keys[4], (LAYERS, STEPS, TOKENS, TOPK), ((0, 4), (2, 8)), -0.2, 0.2), 0.5, 1.5)
    scores_b = jnp.clip(0.5 + 1.0 * jax.random.uniform(keys[5], (LAYERS, STEPS, TOKENS, TOPK), jnp.float32) ** block_levels(keys[5], (LAYERS, STEPS, TOKENS, TOPK), ((0, 4), (2, 8)), -0.2, 0.2), 0.5, 1.5)
    norm_gain = jnp.clip(1.0 + 0.18 * jax.random.normal(keys[6], (LAYERS, D), jnp.float32), 0.1, 1.9)
    w_gate = normal_values(keys[7], (LAYERS, D, EXPERTS * FFE), D ** -0.5, 0.09375, ((0, 4), (2, 8)))
    w_up = normal_values(keys[8], (LAYERS, D, EXPERTS * FFE), D ** -0.5, 0.09375, ((0, 4), (2, 8)))
    w_down = normal_values(keys[9], (LAYERS, EXPERTS * FFE, D), FFE ** -0.5, 0.1875, ((0, 4), (1, 8)))
    return {"flight_a": flight_a, "flight_b": flight_b, "routes_a": routes_a, "routes_b": routes_b, "scores_a": scores_a, "scores_b": scores_b, "norm_gain": norm_gain, "w_gate": w_gate, "w_up": w_up, "w_down": w_down}


EPSILON = 1e-06

def rms_norm(current, gain):
    as_float = current.astype(jnp.float32)
    inverse_rms = lax.rsqrt(lax.optimization_barrier(jnp.mean(as_float * as_float, axis=-1, keepdims=True)) + EPSILON)
    return (as_float * inverse_rms * gain).astype(jnp.bfloat16)

def moe_layer(current, expert_ids, route_weights, gain, gate_rows, up_rows, down_rows):
    normed = rms_norm(current, gain)
    row_limit = N_EP * CAP
    slice_width = FFE // ES
    feature_width = current.shape[1]

    def add_expert(total_out, expert):
        chosen = expert_ids == expert
        coefficient = lax.optimization_barrier(jnp.sum(jnp.where(chosen, route_weights, 0.0), axis=1))
        routed = jnp.any(chosen, axis=1)
        token_index = jnp.nonzero(routed, size=row_limit, fill_value=0)[0].astype(jnp.int32)
        valid_rows = jnp.arange(row_limit, dtype=jnp.int32) < jnp.sum(routed.astype(jnp.int32))
        gathered = normed[token_index]
        gate_cols = lax.dynamic_slice_in_dim(gate_rows, expert * FFE, FFE, 1)
        up_cols = lax.dynamic_slice_in_dim(up_rows, expert * FFE, FFE, 1)
        down_part = lax.dynamic_slice_in_dim(down_rows, expert * FFE, FFE, 0)
        gate_act = jnp.dot(gathered, gate_cols, preferred_element_type=jnp.float32)
        up_act = jnp.dot(gathered, up_cols, preferred_element_type=jnp.float32)
        hidden = (jax.nn.silu(gate_act) * up_act).astype(jnp.bfloat16)
        summed = jnp.zeros((row_limit, feature_width), jnp.float32)
        for piece in range(ES):
            partial_value = jnp.dot(hidden[:, piece * slice_width:(piece + 1) * slice_width], down_part[piece * slice_width:(piece + 1) * slice_width], preferred_element_type=jnp.float32)
            rounded = lax.optimization_barrier(partial_value.astype(jnp.bfloat16))
            summed = summed + rounded.astype(jnp.float32)
        scale_rows = jnp.where(valid_rows, coefficient[token_index], 0.0)
        return (total_out.at[token_index].add(summed * scale_rows[:, None]), None)
    moe_out, _ = lax.scan(add_expert, jnp.zeros(current.shape, jnp.float32), jnp.arange(EXPERTS, dtype=jnp.int32))
    return (current.astype(jnp.float32) + moe_out).astype(jnp.bfloat16)

def reference(flight_a, flight_b, routes_a, routes_b, scores_a, scores_b, norm_gain, w_gate, w_up, w_down):
    results_a = [None] * LAYERS
    results_b = [None] * LAYERS
    for start_section in range(LAYERS):
        current = flight_a[start_section]
        for step_index in range(STEPS):
            layer_index = start_section + step_index
            if layer_index < LAYERS:
                current = moe_layer(current, routes_a[layer_index, step_index], scores_a[layer_index, step_index], norm_gain[layer_index], w_gate[layer_index], w_up[layer_index], w_down[layer_index])
        results_a[(start_section + STEPS) % LAYERS] = current
        current = flight_b[start_section]
        for step_index in range(STEPS):
            layer_index = start_section - step_index
            if layer_index >= 0:
                current = moe_layer(current, routes_b[layer_index, step_index], scores_b[layer_index, step_index], norm_gain[layer_index], w_gate[layer_index], w_up[layer_index], w_down[layer_index])
        results_b[(start_section - STEPS) % LAYERS] = current
    return (jnp.stack(results_a), jnp.stack(results_b))
```

```python
import functools

import jax
import jax.numpy as jnp
from jax import lax
from jax.experimental import pallas as pl
from jax.experimental.pallas import tpu as pltpu
from jax.sharding import PartitionSpec as P

ES = 4
TOPK = 1
CORES = 2
PAIR = ES // CORES

EPSILON = 1e-06
MESH = pl.DeviceIdType.MESH
LANES = 128


def chunk_width(feature_width, most):
    return max(w for w in range(128, most + 1, 128) if feature_width % w == 0)


def window_kernel(
    ep_count,
    section_count,
    fa_whole,
    fb_whole,
    ra,
    rb,
    sa,
    sb,
    gain,
    w_gate,
    w_up,
    w_down,
    out_a,
    out_b,
    fa,
    fb,
    wg,
    wu,
    wd,
    info_out,
    info_in,
    scale_by,
    score_by,
    pick,
    place_home,
    raw_in,
    gath,
    leave,
    acc_g,
    acc_u,
    hid,
    part_out,
    part_in,
    keep,
    home_out,
    home_in,
    final,
    w_sem,
    f_sem,
    w_send,
    w_recv,
    i_send,
    i_recv,
    r_send,
    r_recv,
    l_send,
    l_recv,
    p_send,
    p_recv,
    h_send,
    h_recv,
    z_send,
    z_recv,
):
    groups = ep_count // ES
    chunks, tok, width = fa.shape
    features = chunks * width
    rows = gath.shape[2] // (2 * groups)
    plane = 2 * rows
    pieces = width // LANES
    both = 2 * tok
    sec = lax.axis_index("section")
    me = lax.axis_index("ep")
    group = me // ES
    pair = (me // CORES) % PAIR
    core = me % CORES
    wholes, flights, outs = (fa_whole, fb_whole), (fa, fb), (out_a, out_b)

    def at(g, p, c):
        return (sec, g * ES + p * CORES + c)

    def group_at(i):
        return lax.rem(group + i, groups)

    partner = at(group, pair, 1 - core)
    across = at(group, 1 - pair, core)
    after = (lax.rem(sec + 1, section_count), me)
    before = (lax.rem(sec + section_count - 1, section_count), me)

    barrier = pltpu.get_barrier_semaphore()
    peers = [partner, across, after, before]
    peers += [at(group_at(i), pair, core) for i in range(1, groups)]
    for peer in peers:
        pl.semaphore_signal(barrier, inc=1, device_id=peer, device_id_type=MESH)

    def lanes(k):
        return pl.ds(pl.multiple_of(k * width, LANES), width)

    def flight_load(f, k):
        return pltpu.make_async_copy(wholes[f].at[:, lanes(k)], flights[f].at[k], f_sem.at[f, k])

    for f in range(2):
        lax.fori_loop(0, chunks, lambda k, _, f=f: flight_load(f, k).start() or 0, 0)
    hidden = wg.shape[2]
    own_half, other_half = pl.ds(0, hidden), pl.ds(hidden, hidden)
    weights = (
        (w_gate.at[0], wg.at[0], wg.at[1]),
        (w_up.at[0], wu.at[0], wu.at[1]),
        (w_down.at[0], wd.at[own_half], wd.at[other_half]),
    )
    loads = [
        pltpu.make_async_copy(src, dst, w_sem.at[n]) for n, (src, dst, _) in enumerate(weights)
    ]
    for load in loads:
        load.start()

    def remote(src, dst, send, recv, device):
        return pltpu.make_async_remote_copy(
            src_ref=src,
            dst_ref=dst,
            send_sem=send,
            recv_sem=recv,
            device_id=device,
            device_id_type=MESH,
        )

    def span(i):
        return pl.ds(i * plane, plane)

    def send_weights():
        return [
            remote(src, dst, w_send.at[n], w_recv.at[n], partner)
            for n, (_, src, dst) in enumerate(weights)
        ]

    def info(f):
        return remote(info_out.at[f], info_in.at[f], i_send.at[f], i_recv.at[f], across)

    def raw(f, k):
        return remote(
            flights[f].at[k], raw_in.at[f, k], r_send.at[f, k], r_recv.at[f, k], across
        )

    def leaving(i, f, k):
        return remote(
            leave.at[f, k, span(i - 1)],
            gath.at[f, k, span(groups - i)],
            l_send.at[f, i - 1, k],
            l_recv.at[f, groups - i - 1, k],
            at(group_at(i), pair, core),
        )

    def part(f, k):
        return remote(part_out.at[f, k], part_in.at[f, k], p_send.at[f, k], p_recv.at[f, k], across)

    def homeward(i, f, k):
        return remote(
            home_out.at[f, i - 1, k],
            home_in.at[f, groups - i - 1, k],
            h_send.at[f, i - 1, k],
            h_recv.at[f, groups - i - 1, k],
            at(group_at(i), pair, core),
        )

    def result(f, k):
        return remote(
            final.at[f, k],
            outs[f].at[:, lanes(k)],
            z_send.at[f, k],
            z_recv.at[f, k],
            (after, before)[f],
        )

    pl.semaphore_wait(barrier, len(peers))
    upfront = min(8, chunks)
    ahead = min(1, upfront)

    def loaded(f, k):
        flight_load(f, k).wait()
        if f == 0:
            pl.when(k < ahead)(lambda: raw(0, k).start())
        return 0

    first = lax.broadcasted_iota(jnp.int32, (tok, tok), 0)
    second = lax.broadcasted_iota(jnp.int32, (tok, tok), 1)
    diagonal = first == second
    earlier = jnp.where(first < second, 1.0, 0.0).astype(jnp.bfloat16)
    padded = -(-groups // 8) * 8

    def codes(routes):
        rel = routes - group
        rel = jnp.where(rel < 0, rel + groups, rel)
        named = rel == lax.broadcasted_iota(jnp.int32, (padded, tok), 0)
        named_f = jnp.where(named, 1.0, 0.0)
        count = jnp.dot(
            named_f.astype(jnp.bfloat16), earlier, preferred_element_type=jnp.float32
        )
        slot = jnp.sum(count * named_f, axis=0, keepdims=True)
        return rel.astype(jnp.float32) * plane + slot

    def column(row):
        return jnp.sum(jnp.where(diagonal, row, 0.0), axis=1, keepdims=True)

    def inverse_rms(ref):
        def add(k, total):
            for n in range(pieces):
                v = ref[k, :, n * LANES : (n + 1) * LANES].astype(jnp.float32)
                total += v * v
            return total

        total = lax.fori_loop(0, chunks, add, jnp.zeros((tok, LANES), jnp.float32))
        total = jnp.sum(total, axis=1, keepdims=True)
        return lax.rsqrt(total / features + EPSILON)

    def describe(f):
        lax.fori_loop(0, chunks, lambda k, _: loaded(f, k), 0)
        inv = inverse_rms(flights[f])
        scale_by[f, 0:tok] = jnp.broadcast_to(inv, (tok, LANES))
        info_out[f, 0:1] = codes((ra, rb)[f][...])
        info_out[f, 1:2] = jnp.sum(jnp.where(diagonal, inv, 0.0), axis=0, keepdims=True)
        info(f).start()

    def prepare(f):
        info(f).wait_recv()
        scale_by[f, tok:both] = jnp.broadcast_to(column(info_in[f, 1:2]), (tok, LANES))
        own, other = info_out[f, 0:1], info_in[f, 0:1] + rows
        code = jnp.concatenate([own, other], axis=1).astype(jnp.int32)
        pick[f] = jnp.where(
            code == lax.broadcasted_iota(jnp.int32, (groups * plane, both), 0), 1.0, 0.0
        ).astype(jnp.bfloat16)

    def prepare_return(f):
        own = column(info_out[f, 0:1]).astype(jnp.int32)
        score_by[f] = jnp.broadcast_to(column((sa, sb)[f][...]), (tok, LANES))
        lane = lax.broadcasted_iota(jnp.int32, (tok, pieces * rows), 1)
        for i in range(groups):
            for n in range(pieces):
                held = (own - i * plane == lane - n * rows) & (lane >= n * rows)
                place_home[f, i, n] = jnp.where(
                    held & (lane < (n + 1) * rows), 1.0, 0.0
                ).astype(jnp.bfloat16)

    def wide(value):
        return jnp.concatenate([value] * pieces, axis=1)

    def process(f, k):
        raw(f, k).wait_recv()
        states = jnp.concatenate(
            [flights[f][k].astype(jnp.float32), raw_in[f, k].astype(jnp.float32)], axis=0
        )
        normed = (states * wide(scale_by[f]) * gain[:, lanes(k)]).astype(jnp.bfloat16)
        picked = jnp.dot(pick[f], normed, preferred_element_type=jnp.float32).astype(jnp.bfloat16)
        leave[f, k] = picked[plane:]
        for i in range(1, groups):
            leaving(i, f, k).start()
        gath[f, k, 0:plane] = picked[:plane]

    def project(f, k):
        for i in range(1, groups):
            leaving(i, f, k).wait_recv()
        block = gath[f, k]
        for side in range(CORES):
            rows_of = pl.ds(pl.multiple_of(k * width, LANES), width)
            acc_g[f, side] += jnp.dot(
                block, wg[side, rows_of, :], preferred_element_type=jnp.float32
            )
            acc_u[f, side] += jnp.dot(
                block, wu[side, rows_of, :], preferred_element_type=jnp.float32
            )

    def activate(f):
        for side in range(CORES):
            g = acc_g[f, side]
            hid[f, :, side * hidden : (side + 1) * hidden] = (
                g / (1.0 + jnp.exp(-g)) * acc_u[f, side]
            ).astype(jnp.bfloat16)

    def down(f, k):
        return jnp.dot(hid[f], wd[:, lanes(k)], preferred_element_type=jnp.float32)

    def side_rows(total, s):
        at_row = s * rows
        return jnp.concatenate(
            [total[i * plane + at_row : i * plane + at_row + rows] for i in range(groups)], axis=0
        )

    def send_part(f, k):
        total = down(f, k)
        part_out[f, k] = side_rows(total, 1).astype(jnp.bfloat16)
        part(f, k).start()
        keep[f, k] = side_rows(total, 0)

    def send_home(f, k):
        part(f, k).wait_recv()
        total = keep[f, k] + part_in[f, k].astype(jnp.float32)
        for i in range(1, groups):
            block = total[i * rows : (i + 1) * rows]
            home_out[f, i - 1, k] = jnp.concatenate(
                [block[:, n * LANES : (n + 1) * LANES] for n in range(pieces)], axis=0
            ).astype(jnp.bfloat16)
            homeward(i, f, k).start()
        keep[f, k, 0:rows] = total[0:rows]

    def finish(f, k, moe):
        state = flights[f][k].astype(jnp.float32)
        final[f, k] = (state + moe * wide(score_by[f])).astype(jnp.bfloat16)
        result(f, k).start()

    def finish_home(f, k):
        for i in range(1, groups):
            homeward(groups - i, f, k).wait_recv()
        here = keep[f, k, 0:rows].astype(jnp.bfloat16)
        moe = jnp.dot(
            place_home[f, 0, 0, :, 0:rows], here, preferred_element_type=jnp.float32
        )
        for i in range(1, groups):
            arrived = home_in[f, i - 1, k]
            moe += jnp.concatenate(
                [
                    jnp.dot(place_home[f, i, n], arrived, preferred_element_type=jnp.float32)
                    for n in range(pieces)
                ],
                axis=1,
            )
        finish(f, k, moe)

    def arm(f):
        def zero(side):
            acc_g[f, side] = jnp.zeros(acc_g.shape[2:], jnp.float32)
            acc_u[f, side] = jnp.zeros(acc_u.shape[2:], jnp.float32)

        for side in range(CORES):
            zero(side)

    def weights_here():
        for copy in send_weights():
            copy.wait_recv()

    describe(0)
    lax.fori_loop(ahead, upfront, lambda k, _: raw(0, k).start() or 0, 0)
    for load in loads:
        load.wait()
    for copy in send_weights():
        copy.start()
    prepare(0)

    def describe_b():
        describe(1)
        arm(0)

    def rest():
        prepare(1)
        arm(1)
        prepare_return(0)
        prepare_return(1)


    def once(act):
        return lambda k: act()

    late = 2 * chunks - upfront

    def later(n):
        k = n + upfront

        @pl.when(k < chunks)
        def _():
            raw(0, k).start()

        @pl.when(k >= chunks)
        def _():
            raw(1, k - chunks).start()

    project_a, project_b = 5, chunks + 5
    part_a, part_b = project_a + chunks - 1 + 1, project_b + chunks - 1 + 0
    home_a, home_b = part_a + 2, part_b + 6
    schedule = [
        (2, late, later),
        (1, 1, once(describe_b)),
        (9, 1, once(rest)),
        (0, chunks, lambda k: process(0, k)),
        (chunks, chunks, lambda k: process(1, k)),
        (project_a, 1, once(weights_here)),
        (project_a, chunks, lambda k: project(0, k)),
        (project_a + chunks - 1, 1, once(lambda: activate(0))),
        (part_a, chunks, lambda k: send_part(0, k)),
        (project_b, chunks, lambda k: project(1, k)),
        (project_b + chunks - 1, 1, once(lambda: activate(1))),
        (part_b, chunks, lambda k: send_part(1, k)),
        (home_a, chunks, lambda k: send_home(0, k)),
        (home_a + 3, chunks, lambda k: finish_home(0, k)),
        (home_b, chunks, lambda k: send_home(1, k)),
        (home_b + 2, chunks, lambda k: finish_home(1, k)),
    ]

    def tick(t, _):
        for start, count, act in schedule:

            @pl.when((t >= start) & (t < start + count))
            def _(start=start, act=act):
                act(t - start)

        return 0

    lax.fori_loop(0, max(start + count for start, count, _ in schedule), tick, 0)


    for f in range(2):
        info(f).wait_send()
    for copy in send_weights():
        copy.wait_send()

    def drain(k, _):
        for f in range(2):
            raw(f, k).wait_send()
            for i in range(1, groups):
                leaving(i, f, k).wait_send()
                homeward(i, f, k).wait_send()
            part(f, k).wait_send()
            result(f, k).wait()
        return 0

    lax.fori_loop(0, chunks, drain, 0)

def on_device(
    flight_a, flight_b, routes_a, routes_b, scores_a, scores_b, norm_gain, w_gate, w_up, w_down
):
    ep_count = lax.axis_size("ep")
    section_count = lax.axis_size("section")
    groups = ep_count // ES
    tok, features = flight_a.shape[1:]
    hidden = w_gate.shape[2]
    capacity = min(tok, 9 * tok * TOPK * ES // (8 * ep_count))
    rows = -(-capacity // 8) * 8
    plane = 2 * rows
    width = chunk_width(features, 256)
    chunks = features // width
    pieces = width // LANES
    bf16, f32 = jnp.bfloat16, jnp.float32
    others = groups - 1
    dma = pltpu.SemaphoreType.DMA
    vmem = pl.BlockSpec(memory_space=pltpu.VMEM)
    anywhere = pl.BlockSpec(memory_space=pl.ANY)
    out_a, out_b = pl.pallas_call(
        functools.partial(window_kernel, ep_count, section_count),
        out_shape=(
            pltpu.VMEM((tok, features), bf16),
            pltpu.VMEM((tok, features), bf16),
        ),
        in_specs=[anywhere] * 2 + [vmem] * 5 + [anywhere] * 3,
        out_specs=(vmem, vmem),
        scratch_shapes=[
            pltpu.VMEM((chunks, tok, width), bf16),
            pltpu.VMEM((chunks, tok, width), bf16),
            pltpu.VMEM((CORES, features, hidden), bf16),
            pltpu.VMEM((CORES, features, hidden), bf16),
            pltpu.VMEM((CORES * hidden, features), bf16),
            pltpu.VMEM((2, 2, tok), f32),
            pltpu.VMEM((2, 2, tok), f32),
            pltpu.VMEM((2, 2 * tok, LANES), f32),
            pltpu.VMEM((2, tok, LANES), f32),
            pltpu.VMEM((2, groups * plane, 2 * tok), bf16),
            pltpu.VMEM((2, groups, pieces, tok, pieces * rows), bf16),
            pltpu.VMEM((2, chunks, tok, width), bf16),
            pltpu.VMEM((2, chunks, groups * plane, width), bf16),
            pltpu.VMEM((2, chunks, others * plane, width), bf16),
            pltpu.VMEM((2, CORES, groups * plane, hidden), f32),
            pltpu.VMEM((2, CORES, groups * plane, hidden), f32),
            pltpu.VMEM((2, groups * plane, CORES * hidden), bf16),
            pltpu.VMEM((2, chunks, groups * rows, width), bf16),
            pltpu.VMEM((2, chunks, groups * rows, width), bf16),
            pltpu.VMEM((2, chunks, groups * rows, width), f32),
            pltpu.VMEM((2, others, chunks, pieces * rows, LANES), bf16),
            pltpu.VMEM((2, others, chunks, pieces * rows, LANES), bf16),
            pltpu.VMEM((2, chunks, tok, width), bf16),
            dma((3,)),
            dma((2, chunks)),
            dma((3,)),
            dma((3,)),
            dma((2,)),
            dma((2,)),
            dma((2, chunks)),
            dma((2, chunks)),
            dma((2, others, chunks)),
            dma((2, others, chunks)),
            dma((2, chunks)),
            dma((2, chunks)),
            dma((2, others, chunks)),
            dma((2, others, chunks)),
            dma((2, chunks)),
            dma((2, chunks)),
        ],
        compiler_params=pltpu.CompilerParams(
            collective_id=0, has_side_effects=True, vmem_limit_bytes=62 * 1024 * 1024
        ),
    )(
        flight_a[0],
        flight_b[0],
        routes_a.reshape(1, tok),
        routes_b.reshape(1, tok),
        scores_a.reshape(1, tok),
        scores_b.reshape(1, tok),
        norm_gain,
        w_gate,
        w_up,
        w_down,
    )
    return (out_a[None], out_b[None])


def solution(mesh):
    placed = (
        P("section", "ep", None),
        P("section", "ep", None),
        P("section", None, "ep", None),
        P("section", None, "ep", None),
        P("section", None, "ep", None),
        P("section", None, "ep", None),
        P("section", None),
        P("section", None, "ep"),
        P("section", None, "ep"),
        P("section", "ep", None),
    )
    return jax.shard_map(
        on_device,
        mesh=mesh,
        in_specs=placed,
        out_specs=(P("section", "ep", None), P("section", "ep", None)),
        check_vma=False,
    )
```

```python
import functools

import jax
import jax.numpy as jnp
from jax import lax
from jax.experimental import pallas as pl
from jax.experimental.pallas import tpu as pltpu
from jax.sharding import PartitionSpec as P

ES = 4
TOPK = 1
CORES = 2
PAIR = ES // CORES

EPSILON = 1e-06
MESH = pl.DeviceIdType.MESH
LANES = 128


def chunk_width(feature_width, most):
    return max(w for w in range(128, most + 1, 128) if feature_width % w == 0)


def window_kernel(
    ep_count,
    section_count,
    fa_whole,
    fb_whole,
    ra,
    rb,
    sa,
    sb,
    gain,
    w_gate,
    w_up,
    w_down,
    out_a,
    out_b,
    fa,
    fb,
    wg,
    wu,
    wd,
    info_out,
    info_in,
    scale_by,
    score_by,
    pick,
    place_home,
    raw_in,
    gath,
    leave,
    acc_g,
    acc_u,
    hid,
    part_out,
    part_in,
    keep,
    home_out,
    home_in,
    final,
    w_sem,
    f_sem,
    w_send,
    w_recv,
    i_send,
    i_recv,
    r_send,
    r_recv,
    l_send,
    l_recv,
    p_send,
    p_recv,
    h_send,
    h_recv,
    z_send,
    z_recv,
):
    groups = ep_count // ES
    chunks, tok, width = fa.shape
    features = chunks * width
    rows = gath.shape[2] // (2 * groups)
    plane = 2 * rows
    pieces = width // LANES
    both = 2 * tok
    sec = lax.axis_index("section")
    me = lax.axis_index("ep")
    group = me // ES
    pair = (me // CORES) % PAIR
    core = me % CORES
    wholes, flights, outs = (fa_whole, fb_whole), (fa, fb), (out_a, out_b)

    def at(g, p, c):
        return (sec, g * ES + p * CORES + c)

    def group_at(i):
        return lax.rem(group + i, groups)

    partner = at(group, pair, 1 - core)
    across = at(group, 1 - pair, core)
    after = (lax.rem(sec + 1, section_count), me)
    before = (lax.rem(sec + section_count - 1, section_count), me)

    barrier = pltpu.get_barrier_semaphore()
    peers = [partner, across, after, before]
    peers += [at(group_at(i), pair, core) for i in range(1, groups)]
    for peer in peers:
        pl.semaphore_signal(barrier, inc=1, device_id=peer, device_id_type=MESH)

    def lanes(k):
        return pl.ds(pl.multiple_of(k * width, LANES), width)

    def flight_load(f, k):
        return pltpu.make_async_copy(wholes[f].at[:, lanes(k)], flights[f].at[k], f_sem.at[f, k])

    for f in range(2):
        lax.fori_loop(0, chunks, lambda k, _, f=f: flight_load(f, k).start() or 0, 0)
    hidden = wg.shape[2]
    own_half, other_half = pl.ds(0, hidden), pl.ds(hidden, hidden)
    weights = (
        (w_gate.at[0], wg.at[0], wg.at[1]),
        (w_up.at[0], wu.at[0], wu.at[1]),
        (w_down.at[0], wd.at[own_half], wd.at[other_half]),
    )
    loads = [
        pltpu.make_async_copy(src, dst, w_sem.at[n]) for n, (src, dst, _) in enumerate(weights)
    ]
    for load in loads:
        load.start()

    def remote(src, dst, send, recv, device):
        return pltpu.make_async_remote_copy(
            src_ref=src,
            dst_ref=dst,
            send_sem=send,
            recv_sem=recv,
            device_id=device,
            device_id_type=MESH,
        )

    def span(i):
        return pl.ds(i * plane, plane)

    def send_weights():
        return [
            remote(src, dst, w_send.at[n], w_recv.at[n], partner)
            for n, (_, src, dst) in enumerate(weights)
        ]

    def info(f):
        return remote(info_out.at[f], info_in.at[f], i_send.at[f], i_recv.at[f], across)

    def raw(f, k):
        return remote(
            flights[f].at[k], raw_in.at[f, k], r_send.at[f, k], r_recv.at[f, k], across
        )

    def raw_early(k):
        return remote(
            fa_whole.at[:, lanes(k)], raw_in.at[0, k], r_send.at[0, k], r_recv.at[0, k], across
        )

    def leaving(i, f, k):
        return remote(
            leave.at[f, k, span(i - 1)],
            gath.at[f, k, span(groups - i)],
            l_send.at[f, i - 1, k],
            l_recv.at[f, groups - i - 1, k],
            at(group_at(i), pair, core),
        )

    def part(f, k):
        return remote(part_out.at[f, k], part_in.at[f, k], p_send.at[f, k], p_recv.at[f, k], across)

    def homeward(i, f, k):
        return remote(
            home_out.at[f, i - 1, k],
            home_in.at[f, groups - i - 1, k],
            h_send.at[f, i - 1, k],
            h_recv.at[f, groups - i - 1, k],
            at(group_at(i), pair, core),
        )

    def result(f, k):
        return remote(
            final.at[f, k],
            outs[f].at[:, lanes(k)],
            z_send.at[f, k],
            z_recv.at[f, k],
            (after, before)[f],
        )

    pl.semaphore_wait(barrier, len(peers))
    upfront = min(6, chunks)
    ahead = min(2, upfront)
    lax.fori_loop(0, ahead, lambda k, _: raw_early(k).start() or 0, 0)

    def loaded(f, k):
        flight_load(f, k).wait()
        return 0

    first = lax.broadcasted_iota(jnp.int32, (tok, tok), 0)
    second = lax.broadcasted_iota(jnp.int32, (tok, tok), 1)
    diagonal = first == second
    earlier = jnp.where(first < second, 1.0, 0.0).astype(jnp.bfloat16)
    padded = -(-groups // 8) * 8

    def codes(routes):
        rel = routes - group
        rel = jnp.where(rel < 0, rel + groups, rel)
        named = rel == lax.broadcasted_iota(jnp.int32, (padded, tok), 0)
        named_f = jnp.where(named, 1.0, 0.0)
        count = jnp.dot(
            named_f.astype(jnp.bfloat16), earlier, preferred_element_type=jnp.float32
        )
        slot = jnp.sum(count * named_f, axis=0, keepdims=True)
        return rel.astype(jnp.float32) * plane + slot

    def column(row):
        return jnp.sum(jnp.where(diagonal, row, 0.0), axis=1, keepdims=True)

    def inverse_rms(ref):
        def add(k, total):
            for n in range(pieces):
                v = ref[k, :, n * LANES : (n + 1) * LANES].astype(jnp.float32)
                total += v * v
            return total

        total = lax.fori_loop(0, chunks, add, jnp.zeros((tok, LANES), jnp.float32))
        total = jnp.sum(total, axis=1, keepdims=True)
        return lax.rsqrt(total / features + EPSILON)

    def describe(f):
        lax.fori_loop(0, chunks, lambda k, _: loaded(f, k), 0)
        inv = inverse_rms(flights[f])
        scale_by[f, 0:tok] = jnp.broadcast_to(inv, (tok, LANES))
        info_out[f, 0:1] = codes((ra, rb)[f][...])
        info_out[f, 1:2] = jnp.sum(jnp.where(diagonal, inv, 0.0), axis=0, keepdims=True)
        info(f).start()

    def prepare(f):
        info(f).wait_recv()
        scale_by[f, tok:both] = jnp.broadcast_to(column(info_in[f, 1:2]), (tok, LANES))
        own, other = info_out[f, 0:1], info_in[f, 0:1] + rows
        code = jnp.concatenate([own, other], axis=1).astype(jnp.int32)
        pick[f] = jnp.where(
            code == lax.broadcasted_iota(jnp.int32, (groups * plane, both), 0), 1.0, 0.0
        ).astype(jnp.bfloat16)

    def prepare_return(f):
        own = column(info_out[f, 0:1]).astype(jnp.int32)
        score_by[f] = jnp.broadcast_to(column((sa, sb)[f][...]), (tok, LANES))
        lane = lax.broadcasted_iota(jnp.int32, (tok, pieces * rows), 1)
        for i in range(groups):
            for n in range(pieces):
                held = (own - i * plane == lane - n * rows) & (lane >= n * rows)
                place_home[f, i, n] = jnp.where(
                    held & (lane < (n + 1) * rows), 1.0, 0.0
                ).astype(jnp.bfloat16)

    def wide(value):
        return jnp.concatenate([value] * pieces, axis=1)

    def process(f, k):
        raw(f, k).wait_recv()
        states = jnp.concatenate(
            [flights[f][k].astype(jnp.float32), raw_in[f, k].astype(jnp.float32)], axis=0
        )
        normed = (states * wide(scale_by[f]) * gain[:, lanes(k)]).astype(jnp.bfloat16)
        picked = jnp.dot(pick[f], normed, preferred_element_type=jnp.float32).astype(jnp.bfloat16)
        leave[f, k] = picked[plane:]
        for i in range(1, groups):
            leaving(i, f, k).start()
        gath[f, k, 0:plane] = picked[:plane]

    def project(f, k):
        for i in range(1, groups):
            leaving(i, f, k).wait_recv()
        block = gath[f, k]
        for side in range(CORES):
            rows_of = pl.ds(pl.multiple_of(k * width, LANES), width)
            acc_g[f, side] += jnp.dot(
                block, wg[side, rows_of, :], preferred_element_type=jnp.float32
            )
            acc_u[f, side] += jnp.dot(
                block, wu[side, rows_of, :], preferred_element_type=jnp.float32
            )

    def activate(f):
        for side in range(CORES):
            g = acc_g[f, side]
            hid[f, :, side * hidden : (side + 1) * hidden] = (
                g / (1.0 + jnp.exp(-g)) * acc_u[f, side]
            ).astype(jnp.bfloat16)

    def down(f, k):
        return jnp.dot(hid[f], wd[:, lanes(k)], preferred_element_type=jnp.float32)

    def side_rows(total, s):
        at_row = s * rows
        return jnp.concatenate(
            [total[i * plane + at_row : i * plane + at_row + rows] for i in range(groups)], axis=0
        )

    def send_part(f, k):
        total = down(f, k)
        part_out[f, k] = side_rows(total, 1).astype(jnp.bfloat16)
        part(f, k).start()
        keep[f, k] = side_rows(total, 0)

    def send_home(f, k):
        part(f, k).wait_recv()
        total = keep[f, k] + part_in[f, k].astype(jnp.float32)
        for i in range(1, groups):
            block = total[i * rows : (i + 1) * rows]
            home_out[f, i - 1, k] = jnp.concatenate(
                [block[:, n * LANES : (n + 1) * LANES] for n in range(pieces)], axis=0
            ).astype(jnp.bfloat16)
            homeward(i, f, k).start()
        keep[f, k, 0:rows] = total[0:rows]

    def finish(f, k, moe):
        state = flights[f][k].astype(jnp.float32)
        final[f, k] = (state + moe * wide(score_by[f])).astype(jnp.bfloat16)
        result(f, k).start()

    def finish_home(f, k):
        for i in range(1, groups):
            homeward(groups - i, f, k).wait_recv()
        here = keep[f, k, 0:rows].astype(jnp.bfloat16)
        moe = jnp.dot(
            place_home[f, 0, 0, :, 0:rows], here, preferred_element_type=jnp.float32
        )
        for i in range(1, groups):
            arrived = home_in[f, i - 1, k]
            moe += jnp.concatenate(
                [
                    jnp.dot(place_home[f, i, n], arrived, preferred_element_type=jnp.float32)
                    for n in range(pieces)
                ],
                axis=1,
            )
        finish(f, k, moe)

    def arm(f):
        def zero(side):
            acc_g[f, side] = jnp.zeros(acc_g.shape[2:], jnp.float32)
            acc_u[f, side] = jnp.zeros(acc_u.shape[2:], jnp.float32)

        for side in range(CORES):
            zero(side)

    def weights_here():
        for copy in send_weights():
            copy.wait_recv()

    describe(0)
    lax.fori_loop(ahead, upfront, lambda k, _: raw(0, k).start() or 0, 0)
    for load in loads:
        load.wait()
    for copy in send_weights():
        copy.start()
    prepare(0)

    def describe_b():
        describe(1)
        arm(0)

    def rest():
        prepare(1)
        arm(1)
        prepare_return(0)
        prepare_return(1)


    def once(act):
        return lambda k: act()

    late = 2 * chunks - upfront

    def later(n):
        k = n + upfront

        @pl.when(k < chunks)
        def _():
            raw(0, k).start()

        @pl.when(k >= chunks)
        def _():
            raw(1, k - chunks).start()

    project_a, project_b = 4, chunks + 4
    part_a, part_b = project_a + chunks - 1 + 0, project_b + chunks - 1 + 1
    home_a, home_b = part_a + 3, part_b + 5
    schedule = [
        (1, late, later),
        (1, 1, once(describe_b)),
        (9, 1, once(rest)),
        (0, chunks, lambda k: process(0, k)),
        (chunks, chunks, lambda k: process(1, k)),
        (project_a, 1, once(weights_here)),
        (project_a, chunks, lambda k: project(0, k)),
        (project_a + chunks - 1, 1, once(lambda: activate(0))),
        (part_a, chunks, lambda k: send_part(0, k)),
        (project_b, chunks, lambda k: project(1, k)),
        (project_b + chunks - 1, 1, once(lambda: activate(1))),
        (part_b, chunks, lambda k: send_part(1, k)),
        (home_a, chunks, lambda k: send_home(0, k)),
        (home_a + 2, chunks, lambda k: finish_home(0, k)),
        (home_b, chunks, lambda k: send_home(1, k)),
        (home_b + 2, chunks, lambda k: finish_home(1, k)),
    ]

    def tick(t, _):
        for start, count, act in schedule:

            @pl.when((t >= start) & (t < start + count))
            def _(start=start, act=act):
                act(t - start)

        return 0

    lax.fori_loop(0, max(start + count for start, count, _ in schedule), tick, 0)


    for f in range(2):
        info(f).wait_send()
    for copy in send_weights():
        copy.wait_send()

    def drain(k, _):
        for f in range(2):
            raw(f, k).wait_send()
            for i in range(1, groups):
                leaving(i, f, k).wait_send()
                homeward(i, f, k).wait_send()
            part(f, k).wait_send()
            result(f, k).wait()
        return 0

    lax.fori_loop(0, chunks, drain, 0)

def on_device(
    flight_a, flight_b, routes_a, routes_b, scores_a, scores_b, norm_gain, w_gate, w_up, w_down
):
    ep_count = lax.axis_size("ep")
    section_count = lax.axis_size("section")
    groups = ep_count // ES
    tok, features = flight_a.shape[1:]
    hidden = w_gate.shape[2]
    capacity = min(tok, 9 * tok * TOPK * ES // (8 * ep_count))
    rows = -(-capacity // 8) * 8
    plane = 2 * rows
    width = chunk_width(features, 256)
    chunks = features // width
    pieces = width // LANES
    bf16, f32 = jnp.bfloat16, jnp.float32
    others = groups - 1
    dma = pltpu.SemaphoreType.DMA
    vmem = pl.BlockSpec(memory_space=pltpu.VMEM)
    anywhere = pl.BlockSpec(memory_space=pl.ANY)
    out_a, out_b = pl.pallas_call(
        functools.partial(window_kernel, ep_count, section_count),
        out_shape=(
            pltpu.VMEM((tok, features), bf16),
            pltpu.VMEM((tok, features), bf16),
        ),
        in_specs=[anywhere] * 2 + [vmem] * 5 + [anywhere] * 3,
        out_specs=(vmem, vmem),
        scratch_shapes=[
            pltpu.VMEM((chunks, tok, width), bf16),
            pltpu.VMEM((chunks, tok, width), bf16),
            pltpu.VMEM((CORES, features, hidden), bf16),
            pltpu.VMEM((CORES, features, hidden), bf16),
            pltpu.VMEM((CORES * hidden, features), bf16),
            pltpu.VMEM((2, 2, tok), f32),
            pltpu.VMEM((2, 2, tok), f32),
            pltpu.VMEM((2, 2 * tok, LANES), f32),
            pltpu.VMEM((2, tok, LANES), f32),
            pltpu.VMEM((2, groups * plane, 2 * tok), bf16),
            pltpu.VMEM((2, groups, pieces, tok, pieces * rows), bf16),
            pltpu.VMEM((2, chunks, tok, width), bf16),
            pltpu.VMEM((2, chunks, groups * plane, width), bf16),
            pltpu.VMEM((2, chunks, others * plane, width), bf16),
            pltpu.VMEM((2, CORES, groups * plane, hidden), f32),
            pltpu.VMEM((2, CORES, groups * plane, hidden), f32),
            pltpu.VMEM((2, groups * plane, CORES * hidden), bf16),
            pltpu.VMEM((2, chunks, groups * rows, width), bf16),
            pltpu.VMEM((2, chunks, groups * rows, width), bf16),
            pltpu.VMEM((2, chunks, groups * rows, width), f32),
            pltpu.VMEM((2, others, chunks, pieces * rows, LANES), bf16),
            pltpu.VMEM((2, others, chunks, pieces * rows, LANES), bf16),
            pltpu.VMEM((2, chunks, tok, width), bf16),
            dma((3,)),
            dma((2, chunks)),
            dma((3,)),
            dma((3,)),
            dma((2,)),
            dma((2,)),
            dma((2, chunks)),
            dma((2, chunks)),
            dma((2, others, chunks)),
            dma((2, others, chunks)),
            dma((2, chunks)),
            dma((2, chunks)),
            dma((2, others, chunks)),
            dma((2, others, chunks)),
            dma((2, chunks)),
            dma((2, chunks)),
        ],
        compiler_params=pltpu.CompilerParams(
            collective_id=0, has_side_effects=True, vmem_limit_bytes=62 * 1024 * 1024
        ),
    )(
        flight_a[0],
        flight_b[0],
        routes_a.reshape(1, tok),
        routes_b.reshape(1, tok),
        scores_a.reshape(1, tok),
        scores_b.reshape(1, tok),
        norm_gain,
        w_gate,
        w_up,
        w_down,
    )
    return (out_a[None], out_b[None])


def solution(mesh):
    placed = (
        P("section", "ep", None),
        P("section", "ep", None),
        P("section", None, "ep", None),
        P("section", None, "ep", None),
        P("section", None, "ep", None),
        P("section", None, "ep", None),
        P("section", None),
        P("section", None, "ep"),
        P("section", None, "ep"),
        P("section", "ep", None),
    )
    return jax.shard_map(
        on_device,
        mesh=mesh,
        in_specs=placed,
        out_specs=(P("section", "ep", None), P("section", "ep", None)),
        check_vma=False,
    )
```

```python
import functools

import jax
import jax.numpy as jnp
from jax import lax
from jax.experimental import pallas as pl
from jax.experimental.pallas import tpu as pltpu
from jax.sharding import PartitionSpec as P

ES = 4
TOPK = 1
CORES = 2
PAIR = ES // CORES

EPSILON = 1e-06
MESH = pl.DeviceIdType.MESH
LANES = 128


def chunk_width(feature_width, most):
    return max(w for w in range(128, most + 1, 128) if feature_width % w == 0)


def window_kernel(
    ep_count,
    section_count,
    fa_whole,
    fb_whole,
    ra,
    rb,
    sa,
    sb,
    gain,
    w_gate,
    w_up,
    w_down,
    out_a,
    out_b,
    fa,
    fb,
    wg,
    wu,
    wd,
    info_out,
    info_in,
    scale_by,
    score_by,
    pick,
    place_home,
    raw_in,
    gath,
    leave,
    acc_g,
    acc_u,
    hid,
    part_out,
    part_in,
    keep,
    home_out,
    home_in,
    final,
    w_sem,
    f_sem,
    w_send,
    w_recv,
    i_send,
    i_recv,
    r_send,
    r_recv,
    l_send,
    l_recv,
    p_send,
    p_recv,
    h_send,
    h_recv,
    z_send,
    z_recv,
):
    groups = ep_count // ES
    chunks, tok, width = fa.shape
    features = chunks * width
    rows = gath.shape[2] // (2 * groups)
    plane = 2 * rows
    pieces = width // LANES
    both = 2 * tok
    sec = lax.axis_index("section")
    me = lax.axis_index("ep")
    group = me // ES
    pair = (me // CORES) % PAIR
    core = me % CORES
    wholes, flights, outs = (fa_whole, fb_whole), (fa, fb), (out_a, out_b)

    def at(g, p, c):
        return (sec, g * ES + p * CORES + c)

    def group_at(i):
        return lax.rem(group + i, groups)

    partner = at(group, pair, 1 - core)
    across = at(group, 1 - pair, core)
    after = (lax.rem(sec + 1, section_count), me)
    before = (lax.rem(sec + section_count - 1, section_count), me)

    barrier = pltpu.get_barrier_semaphore()
    peers = [partner, across, after, before]
    peers += [at(group_at(i), pair, core) for i in range(1, groups)]
    for peer in peers:
        pl.semaphore_signal(barrier, inc=1, device_id=peer, device_id_type=MESH)

    def lanes(k):
        return pl.ds(pl.multiple_of(k * width, LANES), width)

    def flight_load(f, k):
        return pltpu.make_async_copy(wholes[f].at[:, lanes(k)], flights[f].at[k], f_sem.at[f, k])

    for f in range(2):
        lax.fori_loop(0, chunks, lambda k, _, f=f: flight_load(f, k).start() or 0, 0)
    hidden = wg.shape[2]
    own_half, other_half = pl.ds(0, hidden), pl.ds(hidden, hidden)
    weights = (
        (w_gate.at[0], wg.at[0], wg.at[1]),
        (w_up.at[0], wu.at[0], wu.at[1]),
        (w_down.at[0], wd.at[own_half], wd.at[other_half]),
    )
    loads = [
        pltpu.make_async_copy(src, dst, w_sem.at[n]) for n, (src, dst, _) in enumerate(weights)
    ]
    for load in loads:
        load.start()

    def remote(src, dst, send, recv, device):
        return pltpu.make_async_remote_copy(
            src_ref=src,
            dst_ref=dst,
            send_sem=send,
            recv_sem=recv,
            device_id=device,
            device_id_type=MESH,
        )

    def span(i):
        return pl.ds(i * plane, plane)

    def send_weights():
        return [
            remote(src, dst, w_send.at[n], w_recv.at[n], partner)
            for n, (_, src, dst) in enumerate(weights)
        ]

    def info(f):
        return remote(info_out.at[f], info_in.at[f], i_send.at[f], i_recv.at[f], across)

    def raw(f, k):
        return remote(
            flights[f].at[k], raw_in.at[f, k], r_send.at[f, k], r_recv.at[f, k], across
        )

    def raw_early(k):
        return remote(
            fa_whole.at[:, lanes(k)], raw_in.at[0, k], r_send.at[0, k], r_recv.at[0, k], across
        )

    def leaving(i, f, k):
        return remote(
            leave.at[f, k, span(i - 1)],
            gath.at[f, k, span(groups - i)],
            l_send.at[f, i - 1, k],
            l_recv.at[f, groups - i - 1, k],
            at(group_at(i), pair, core),
        )

    def part(f, k):
        return remote(part_out.at[f, k], part_in.at[f, k], p_send.at[f, k], p_recv.at[f, k], across)

    def homeward(i, f, k):
        return remote(
            home_out.at[f, i - 1, k],
            home_in.at[f, groups - i - 1, k],
            h_send.at[f, i - 1, k],
            h_recv.at[f, groups - i - 1, k],
            at(group_at(i), pair, core),
        )

    def result(f, k):
        return remote(
            final.at[f, k],
            outs[f].at[:, lanes(k)],
            z_send.at[f, k],
            z_recv.at[f, k],
            (after, before)[f],
        )

    pl.semaphore_wait(barrier, len(peers))
    upfront = min(3, chunks)
    ahead = min(1, upfront)
    lax.fori_loop(0, ahead, lambda k, _: raw_early(k).start() or 0, 0)

    def loaded(f, k):
        flight_load(f, k).wait()
        return 0

    first = lax.broadcasted_iota(jnp.int32, (tok, tok), 0)
    second = lax.broadcasted_iota(jnp.int32, (tok, tok), 1)
    diagonal = first == second
    earlier = jnp.where(first < second, 1.0, 0.0).astype(jnp.bfloat16)
    padded = -(-groups // 8) * 8

    def codes(routes):
        rel = routes - group
        rel = jnp.where(rel < 0, rel + groups, rel)
        named = rel == lax.broadcasted_iota(jnp.int32, (padded, tok), 0)
        named_f = jnp.where(named, 1.0, 0.0)
        count = jnp.dot(
            named_f.astype(jnp.bfloat16), earlier, preferred_element_type=jnp.float32
        )
        slot = jnp.sum(count * named_f, axis=0, keepdims=True)
        return rel.astype(jnp.float32) * plane + slot

    def column(row):
        return jnp.sum(jnp.where(diagonal, row, 0.0), axis=1, keepdims=True)

    def inverse_rms(ref):
        def add(k, total):
            for n in range(pieces):
                v = ref[k, :, n * LANES : (n + 1) * LANES].astype(jnp.float32)
                total += v * v
            return total

        total = lax.fori_loop(0, chunks, add, jnp.zeros((tok, LANES), jnp.float32))
        total = jnp.sum(total, axis=1, keepdims=True)
        return lax.rsqrt(total / features + EPSILON)

    def describe(f):
        lax.fori_loop(0, chunks, lambda k, _: loaded(f, k), 0)
        inv = inverse_rms(flights[f])
        scale_by[f, 0:tok] = jnp.broadcast_to(inv, (tok, LANES))
        info_out[f, 0:1] = codes((ra, rb)[f][...])
        info_out[f, 1:2] = jnp.sum(jnp.where(diagonal, inv, 0.0), axis=0, keepdims=True)
        info(f).start()

    def prepare(f):
        info(f).wait_recv()
        scale_by[f, tok:both] = jnp.broadcast_to(column(info_in[f, 1:2]), (tok, LANES))
        own, other = info_out[f, 0:1], info_in[f, 0:1] + rows
        code = jnp.concatenate([own, other], axis=1).astype(jnp.int32)
        pick[f] = jnp.where(
            code == lax.broadcasted_iota(jnp.int32, (groups * plane, both), 0), 1.0, 0.0
        ).astype(jnp.bfloat16)

    def prepare_return(f):
        own = column(info_out[f, 0:1]).astype(jnp.int32)
        score_by[f] = jnp.broadcast_to(column((sa, sb)[f][...]), (tok, LANES))
        lane = lax.broadcasted_iota(jnp.int32, (tok, pieces * rows), 1)
        for i in range(groups):
            for n in range(pieces):
                held = (own - i * plane == lane - n * rows) & (lane >= n * rows)
                place_home[f, i, n] = jnp.where(
                    held & (lane < (n + 1) * rows), 1.0, 0.0
                ).astype(jnp.bfloat16)

    def wide(value):
        return jnp.concatenate([value] * pieces, axis=1)

    def process(f, k):
        raw(f, k).wait_recv()
        states = jnp.concatenate(
            [flights[f][k].astype(jnp.float32), raw_in[f, k].astype(jnp.float32)], axis=0
        )
        normed = (states * wide(scale_by[f]) * gain[:, lanes(k)]).astype(jnp.bfloat16)
        picked = jnp.dot(pick[f], normed, preferred_element_type=jnp.float32).astype(jnp.bfloat16)
        leave[f, k] = picked[plane:]
        for i in range(1, groups):
            leaving(i, f, k).start()
        gath[f, k, 0:plane] = picked[:plane]

    def project(f, k):
        for i in range(1, groups):
            leaving(i, f, k).wait_recv()
        block = gath[f, k]
        for side in range(CORES):
            rows_of = pl.ds(pl.multiple_of(k * width, LANES), width)
            acc_g[f, side] += jnp.dot(
                block, wg[side, rows_of, :], preferred_element_type=jnp.float32
            )
            acc_u[f, side] += jnp.dot(
                block, wu[side, rows_of, :], preferred_element_type=jnp.float32
            )

    def activate(f):
        for side in range(CORES):
            g = acc_g[f, side]
            hid[f, :, side * hidden : (side + 1) * hidden] = (
                g / (1.0 + jnp.exp(-g)) * acc_u[f, side]
            ).astype(jnp.bfloat16)

    def down(f, k):
        return jnp.dot(hid[f], wd[:, lanes(k)], preferred_element_type=jnp.float32)

    def side_rows(total, s):
        at_row = s * rows
        return jnp.concatenate(
            [total[i * plane + at_row : i * plane + at_row + rows] for i in range(groups)], axis=0
        )

    def send_part(f, k):
        total = down(f, k)
        part_out[f, k] = side_rows(total, 1).astype(jnp.bfloat16)
        part(f, k).start()
        keep[f, k] = side_rows(total, 0)

    def send_home(f, k):
        part(f, k).wait_recv()
        total = keep[f, k] + part_in[f, k].astype(jnp.float32)
        for i in range(1, groups):
            block = total[i * rows : (i + 1) * rows]
            home_out[f, i - 1, k] = jnp.concatenate(
                [block[:, n * LANES : (n + 1) * LANES] for n in range(pieces)], axis=0
            ).astype(jnp.bfloat16)
            homeward(i, f, k).start()
        keep[f, k, 0:rows] = total[0:rows]

    def finish(f, k, moe):
        state = flights[f][k].astype(jnp.float32)
        final[f, k] = (state + moe * wide(score_by[f])).astype(jnp.bfloat16)
        result(f, k).start()

    def finish_home(f, k):
        for i in range(1, groups):
            homeward(groups - i, f, k).wait_recv()
        here = keep[f, k, 0:rows].astype(jnp.bfloat16)
        moe = jnp.dot(
            place_home[f, 0, 0, :, 0:rows], here, preferred_element_type=jnp.float32
        )
        for i in range(1, groups):
            arrived = home_in[f, i - 1, k]
            moe += jnp.concatenate(
                [
                    jnp.dot(place_home[f, i, n], arrived, preferred_element_type=jnp.float32)
                    for n in range(pieces)
                ],
                axis=1,
            )
        finish(f, k, moe)

    def arm(f):
        def zero(side):
            acc_g[f, side] = jnp.zeros(acc_g.shape[2:], jnp.float32)
            acc_u[f, side] = jnp.zeros(acc_u.shape[2:], jnp.float32)

        for side in range(CORES):
            zero(side)

    def weights_here():
        for copy in send_weights():
            copy.wait_recv()

    describe(0)
    lax.fori_loop(ahead, upfront, lambda k, _: raw(0, k).start() or 0, 0)
    for load in loads:
        load.wait()
    for copy in send_weights():
        copy.start()
    prepare(0)

    def describe_b():
        describe(1)
        arm(0)

    def rest():
        prepare(1)
        arm(1)
        prepare_return(0)
        prepare_return(1)


    def once(act):
        return lambda k: act()

    late = 2 * chunks - upfront

    def later(n):
        k = n + upfront

        @pl.when(k < chunks)
        def _():
            raw(0, k).start()

        @pl.when(k >= chunks)
        def _():
            raw(1, k - chunks).start()

    project_a, project_b = 2, chunks + 2
    part_a, part_b = project_a + chunks - 1 + 0, project_b + chunks - 1 + 1
    home_a, home_b = part_a + 2, part_b + 2
    schedule = [
        (1, late, later),
        (1, 1, once(describe_b)),
        (4, 1, once(rest)),
        (0, chunks, lambda k: process(0, k)),
        (chunks, chunks, lambda k: process(1, k)),
        (project_a, 1, once(weights_here)),
        (project_a, chunks, lambda k: project(0, k)),
        (project_a + chunks - 1, 1, once(lambda: activate(0))),
        (part_a, chunks, lambda k: send_part(0, k)),
        (project_b, chunks, lambda k: project(1, k)),
        (project_b + chunks - 1, 1, once(lambda: activate(1))),
        (part_b, chunks, lambda k: send_part(1, k)),
        (home_a, chunks, lambda k: send_home(0, k)),
        (home_a + 1, chunks, lambda k: finish_home(0, k)),
        (home_b, chunks, lambda k: send_home(1, k)),
        (home_b + 1, chunks, lambda k: finish_home(1, k)),
    ]

    def tick(t, _):
        for start, count, act in schedule:

            @pl.when((t >= start) & (t < start + count))
            def _(start=start, act=act):
                act(t - start)

        return 0

    lax.fori_loop(0, max(start + count for start, count, _ in schedule), tick, 0)


    for f in range(2):
        info(f).wait_send()
    for copy in send_weights():
        copy.wait_send()

    def drain(k, _):
        for f in range(2):
            raw(f, k).wait_send()
            for i in range(1, groups):
                leaving(i, f, k).wait_send()
                homeward(i, f, k).wait_send()
            part(f, k).wait_send()
            result(f, k).wait()
        return 0

    lax.fori_loop(0, chunks, drain, 0)

def on_device(
    flight_a, flight_b, routes_a, routes_b, scores_a, scores_b, norm_gain, w_gate, w_up, w_down
):
    ep_count = lax.axis_size("ep")
    section_count = lax.axis_size("section")
    groups = ep_count // ES
    tok, features = flight_a.shape[1:]
    hidden = w_gate.shape[2]
    capacity = min(tok, 9 * tok * TOPK * ES // (8 * ep_count))
    rows = -(-capacity // 8) * 8
    plane = 2 * rows
    width = chunk_width(features, 512)
    chunks = features // width
    pieces = width // LANES
    bf16, f32 = jnp.bfloat16, jnp.float32
    others = groups - 1
    dma = pltpu.SemaphoreType.DMA
    vmem = pl.BlockSpec(memory_space=pltpu.VMEM)
    anywhere = pl.BlockSpec(memory_space=pl.ANY)
    out_a, out_b = pl.pallas_call(
        functools.partial(window_kernel, ep_count, section_count),
        out_shape=(
            pltpu.VMEM((tok, features), bf16),
            pltpu.VMEM((tok, features), bf16),
        ),
        in_specs=[anywhere] * 2 + [vmem] * 5 + [anywhere] * 3,
        out_specs=(vmem, vmem),
        scratch_shapes=[
            pltpu.VMEM((chunks, tok, width), bf16),
            pltpu.VMEM((chunks, tok, width), bf16),
            pltpu.VMEM((CORES, features, hidden), bf16),
            pltpu.VMEM((CORES, features, hidden), bf16),
            pltpu.VMEM((CORES * hidden, features), bf16),
            pltpu.VMEM((2, 2, tok), f32),
            pltpu.VMEM((2, 2, tok), f32),
            pltpu.VMEM((2, 2 * tok, LANES), f32),
            pltpu.VMEM((2, tok, LANES), f32),
            pltpu.VMEM((2, groups * plane, 2 * tok), bf16),
            pltpu.VMEM((2, groups, pieces, tok, pieces * rows), bf16),
            pltpu.VMEM((2, chunks, tok, width), bf16),
            pltpu.VMEM((2, chunks, groups * plane, width), bf16),
            pltpu.VMEM((2, chunks, others * plane, width), bf16),
            pltpu.VMEM((2, CORES, groups * plane, hidden), f32),
            pltpu.VMEM((2, CORES, groups * plane, hidden), f32),
            pltpu.VMEM((2, groups * plane, CORES * hidden), bf16),
            pltpu.VMEM((2, chunks, groups * rows, width), bf16),
            pltpu.VMEM((2, chunks, groups * rows, width), bf16),
            pltpu.VMEM((2, chunks, groups * rows, width), f32),
            pltpu.VMEM((2, others, chunks, pieces * rows, LANES), bf16),
            pltpu.VMEM((2, others, chunks, pieces * rows, LANES), bf16),
            pltpu.VMEM((2, chunks, tok, width), bf16),
            dma((3,)),
            dma((2, chunks)),
            dma((3,)),
            dma((3,)),
            dma((2,)),
            dma((2,)),
            dma((2, chunks)),
            dma((2, chunks)),
            dma((2, others, chunks)),
            dma((2, others, chunks)),
            dma((2, chunks)),
            dma((2, chunks)),
            dma((2, others, chunks)),
            dma((2, others, chunks)),
            dma((2, chunks)),
            dma((2, chunks)),
        ],
        compiler_params=pltpu.CompilerParams(
            collective_id=0, has_side_effects=True, vmem_limit_bytes=62 * 1024 * 1024
        ),
    )(
        flight_a[0],
        flight_b[0],
        routes_a.reshape(1, tok),
        routes_b.reshape(1, tok),
        scores_a.reshape(1, tok),
        scores_b.reshape(1, tok),
        norm_gain,
        w_gate,
        w_up,
        w_down,
    )
    return (out_a[None], out_b[None])


def solution(mesh):
    placed = (
        P("section", "ep", None),
        P("section", "ep", None),
        P("section", None, "ep", None),
        P("section", None, "ep", None),
        P("section", None, "ep", None),
        P("section", None, "ep", None),
        P("section", None),
        P("section", None, "ep"),
        P("section", None, "ep"),
        P("section", "ep", None),
    )
    return jax.shard_map(
        on_device,
        mesh=mesh,
        in_specs=placed,
        out_specs=(P("section", "ep", None), P("section", "ep", None)),
        check_vma=False,
    )
```
